256 devices in a mesh: wide: 32 (over y_lo, z, core), narrow: 8 (over x, y_hi).
Axes of the slice: x: 4, y: 4 (y_hi: 2, y_lo: 2; y = y_hi * 2 + y_lo), z: 8, core: 2. Of those that a mesh axis runs over, the one named last changes fastest.
Arguments:
- dark: bfloat16 [64, 32, 8, 16], P(None, None, 'narrow'), may hold values from -6 to 6
- w_enc: bfloat16 [27, 64, 64], replicated, may hold values from -0.15625 to 0.15625
- up_weight: bfloat16 [512, 16, 64], replicated, may hold values from -0.75 to 0.75
- w_dec: bfloat16 [27, 16, 16], replicated, may hold values from -0.3125 to 0.3125
- cotangent: bfloat16 [16, 256, 64, 128], P(None, 'wide', 'narrow'), may hold values from -6 to 6
Outputs:
- grad_dark: float32 [64, 32, 8, 16], P(None, None, 'narrow')
- grad_w_enc: float32 [27, 64, 64], replicated
- grad_up_weight: float32 [512, 16, 64], P(('wide', 'narrow'))
- grad_w_dec: float32 [27, 16, 16], replicated
The draws below stay inside these ranges and needn't reach their ends.
All inputs are finite; a program needn't handle non-finite values.
Results may differ from the reference program's by a relative error of at most 0.0053.
Values may be sent and summed in bfloat16 or wider, within the bound.
A program may use at most 64 MiB of HBM per device.

```python
import math
import jax
import jax.numpy as jnp
from jax import lax

CH = 64
FCH = 16
RATIO = 8
CY = 16
FY = 128
XC = 32
ZC = 8
XF = 256
ZF = 64
SUBS = 512
NCOARSE = 4096
NFINE = 2097152


def steps_of(own_key, dims, pieces, low, top_value):
    loudness = 1.0
    for dim, parts in pieces:
        steps = jax.random.uniform(jax.random.fold_in(jax.random.fold_in(own_key, 6), dim), (parts,), jnp.float32, low / len(pieces), top_value / len(pieces))
        loudness = loudness * jnp.repeat(jnp.exp(steps), dims[dim] // parts).reshape((-1,) + (1,) * (len(dims) - 1 - dim))
    return loudness


def bell_draw(stream_key, dims, spread, bound, shards=(), kind=jnp.bfloat16):
    values = jax.random.normal(stream_key, dims, jnp.float32) * spread
    if len(shards) > 0:
        values = steps_of(stream_key, dims, shards, -0.22, 0.18) * values
    return jnp.clip(values, min=-bound, max=bound).astype(kind)


def setup_inputs(seed: int = 0) -> dict:
    keys = jax.random.split(jax.random.key(seed), 6)
    dark = bell_draw(keys[0], (CH, XC, ZC, CY), 1.0, 6.0, ((2, 8),))
    w_enc = bell_draw(keys[1], (27, CH, CH), (27 * CH) ** -0.5, 0.15625)
    up_weight = bell_draw(keys[2], (SUBS, FCH, CH), CH ** -0.5, 0.75)
    w_dec = bell_draw(keys[3], (27, FCH, FCH), (27 * FCH) ** -0.5, 0.3125)
    cotangent = bell_draw(keys[4], (FCH, XF, ZF, FY), 1.0, 6.0, ((1, 32), (2, 8)))
    return {"dark": dark, "w_enc": w_enc, "up_weight": up_weight, "w_dec": w_dec, "cotangent": cotangent}


def convolve(field, kernel):
    outputs = kernel.shape[1]
    inputs = kernel.shape[2]
    taps = kernel.reshape(3, 3, 3, outputs, inputs).transpose(3, 4, 0, 1, 2)
    result = lax.conv_general_dilated(field[None], taps, (1, 1, 1), ((1, 1), (1, 1), (1, 1)), dimension_numbers=('NCDHW', 'OIDHW', 'NCDHW'), precision=lax.Precision.HIGHEST)
    return result[0]

def silu_slope(values):
    sigma = jax.nn.sigmoid(values)
    return sigma * (1.0 + values * (1.0 - sigma))

def reference(dark, w_enc, up_weight, w_dec, cotangent):
    ratio = RATIO
    dark_float = dark.astype(jnp.float32)
    enc_kernel = w_enc.astype(jnp.float32)
    enc_pre = convolve(dark_float, enc_kernel)
    encoded = jax.nn.silu(enc_pre).astype(jnp.bfloat16)
    planes = encoded.shape[1]
    depth = encoded.shape[2]
    width = encoded.shape[3]
    table = up_weight.astype(jnp.float32).reshape(ratio, ratio, ratio, FCH, CH)
    enc_float = encoded.astype(jnp.float32)
    upsampled = jnp.einsum('ijkoc,cxzy->oxizjyk', table, enc_float).reshape(FCH, planes * ratio, depth * ratio, width * ratio).astype(jnp.bfloat16)
    up_float = upsampled.astype(jnp.float32)
    dec_kernel = w_dec.astype(jnp.float32)
    dec_pre = convolve(up_float, dec_kernel)
    cot_float = cotangent.astype(jnp.float32)
    dec_grad = (cot_float * silu_slope(dec_pre)).astype(jnp.bfloat16)
    _, pull_fine = jax.vjp(convolve, up_float, dec_kernel)
    back_up, grad_dec = pull_fine(dec_grad.astype(jnp.float32))
    up_grad = (cot_float + back_up).astype(jnp.bfloat16)
    grad_blocks = up_grad.astype(jnp.float32).reshape(FCH, planes, ratio, depth, ratio, width, ratio)
    grad_up = jnp.einsum('oxizjyk,cxzy->ijkoc', grad_blocks, enc_float).reshape(ratio * ratio * ratio, FCH, CH)
    enc_grad = jnp.einsum('ijkoc,oxizjyk->cxzy', table, grad_blocks).astype(jnp.bfloat16)
    enc_pre_grad = (enc_grad.astype(jnp.float32) * silu_slope(enc_pre)).astype(jnp.bfloat16)
    _, pull_coarse = jax.vjp(convolve, dark_float, enc_kernel)
    grad_dark, grad_enc = pull_coarse(enc_pre_grad.astype(jnp.float32))
    coarse_scale = 1.0 / math.sqrt(NCOARSE)
    fine_scale = 1.0 / math.sqrt(NFINE)
    return (grad_dark, grad_enc * coarse_scale, grad_up * coarse_scale, grad_dec * fine_scale)
```

```python
import math

import jax
import jax.numpy as jnp
from jax import lax
from jax.experimental import pallas as pl
from jax.experimental.pallas import tpu as pltpu
from jax.sharding import PartitionSpec as P

MESH = pl.DeviceIdType.MESH
BF = jnp.bfloat16
F32 = jnp.float32
NW = 32
NN = 8
RATIO = 8
CH = 64
FCH = 16


def dot_nt(a, b):
    return lax.dot_general(a, b, (((1,), (1,)), ((), ())), preferred_element_type=F32)


def dot_nn(a, b):
    return lax.dot_general(a, b, (((1,), (0,)), ((), ())), preferred_element_type=F32)


def dot_tn(a, b):
    return lax.dot_general(a, b, (((0,), (0,)), ((), ())), preferred_element_type=F32)


def silu_slope(values):
    sigma = jax.nn.sigmoid(values)
    return sigma * (1.0 + values * (1.0 - sigma))


def iota(shape, dim):
    return lax.broadcasted_iota(jnp.int32, shape, dim)


def mult(value, of):
    return pl.multiple_of(value, of)


def shifted_rows(field):
    rows = field.shape[0]
    y = iota(field.shape, 0) % 16
    low = jnp.where(y == 0, 0.0, pltpu.roll(field, 1, 0))
    high = jnp.where(y == 15, 0.0, pltpu.roll(field, rows - 1, 0))
    return jnp.concatenate([low, field, high], axis=1).astype(BF)


def shifted_lanes(field):
    lane = iota(field.shape, 1)
    low = jnp.where(lane == 0, 0.0, pltpu.roll(field, 1, 1))
    high = jnp.where(lane == 127, 0.0, pltpu.roll(field, 127, 1))
    return low, high


def expand(enc):
    rep = jnp.broadcast_to(enc[:, None, :], (16, 8, 64)).reshape(128, 64)
    wide = jnp.concatenate([rep] * 8, axis=1)
    mask = (iota((128, 512), 0) % 8) == (iota((128, 512), 1) // 64)
    return jnp.where(mask, wide, 0.0).astype(BF)


def remote(src, dst, send, recv, target):
    return pltpu.make_async_remote_copy(
        src_ref=src, dst_ref=dst, send_sem=send, recv_sem=recv, device_id=target, device_id_type=MESH
    )


def kernel(
    dark, we, wd, tab, t1, t2, cot,
    gd_out, ge_out, gu_out, gw_out,
    dark_g, de, cot_p, encx, v, dg, gacc, ug, ur, es, eg, ee, encf, ga, gp, gr,
    h1s, h1r, h2s, h2r, h3s, h3r, h4s, h4r,
    dark_ss, dark_rs, cot_ss, cot_rs, ug_ss, ug_rs, e1_ss, e1_rs, e2_ss, e2_rs,
    gp_ss, gp_rs, h1_ss, h1_rs, h2_ss, h2_rs, h3_ss, h3_rs, h4_ss, h4_rs,
):
    w = lax.axis_index("wide")
    n = lax.axis_index("narrow")
    wl, wr = (w + NW - 1) % NW, (w + 1) % NW
    nl, nr = (n + NN - 1) % NN, (n + 1) % NN
    quad = w // 4
    seat = w % 4

    barrier = pltpu.get_barrier_semaphore()

    def greet(target):
        pl.semaphore_signal(barrier, inc=1, device_id=target, device_id_type=MESH)

    @pl.loop(1, NN)
    def _(d):
        greet({"wide": w, "narrow": (n + d) % NN})

    @pl.loop(1, NW)
    def _(d):
        greet({"wide": (w + d) % NW, "narrow": n})

    for a in (wl, wr):
        for b in (nl, nr):
            greet({"wide": a, "narrow": b})

    dark_g[n] = dark[...]
    for i in range(8):
        cot_p[i + 1, 16:144, :] = cot[i]
    zero_plane = jnp.zeros((576, 192), BF)
    for i in (0, 1, 10, 11):
        de[i] = zero_plane

    @pl.loop(2, 10)
    def _(i):
        de[i, 0:32, :] = jnp.zeros((32, 192), BF)
        de[i, 544:576, :] = jnp.zeros((32, 192), BF)

    zero_coarse = jnp.zeros((512, 64), BF)
    eg[0] = zero_coarse
    eg[9] = zero_coarse
    for i in range(3):
        ee[i, 0:16, :] = jnp.zeros((16, 192), BF)
        ee[i, 528:544, :] = jnp.zeros((16, 192), BF)

    pl.semaphore_wait(barrier, NN - 1 + NW - 1 + 4)

    def dark_copy(d):
        return remote(
            dark, dark_g.at[n], dark_ss.at[d], dark_rs.at[d], {"wide": w, "narrow": (n + d) % NN}
        )

    @pl.loop(1, NN)
    def _(d):
        dark_copy(d).start()

    cot_copies = []
    for dx in (-1, 0, 1):
        for dz in (-1, 0, 1):
            if dx == 0 and dz == 0:
                continue
            tw = (wl, w, wr)[dx + 1]
            tn = (nl, n, nr)[dz + 1]
            sx = {-1: (0, 1), 0: (0, 8), 1: (7, 1)}[dx]
            sz = {-1: (0, 16), 0: (0, 128), 1: (112, 16)}[dz]
            tx = {-1: 9, 0: 1, 1: 0}[dx]
            tz = {-1: 144, 0: 16, 1: 0}[dz]
            index = len(cot_copies)
            cot_copies.append(
                remote(
                    cot.at[pl.ds(sx[0], sx[1]), pl.ds(sz[0], sz[1]), :],
                    cot_p.at[pl.ds(tx, sx[1]), pl.ds(tz, sz[1]), :],
                    cot_ss.at[index],
                    cot_rs.at[index],
                    {"wide": tw, "narrow": tn},
                )
            )
    for copy in cot_copies:
        copy.start()

    @pl.loop(1, NN)
    def _(d):
        dark_copy(d).wait_recv()

    @pl.loop(0, NN)
    def _(z):
        de[z + 2, 32:544, :] = shifted_rows(dark_g[z].astype(F32))

    enc_pre_own = None
    for dz in range(3):
        acc = jnp.zeros((48, 64), F32)
        for a in range(3):
            for b in range(3):
                rows = de[n + dz + b, pl.ds(mult((w + a) * 16, 16), 48), :]
                acc = acc + dot_nt(rows, we[3 * a + b])
        if dz == 1:
            enc_pre_own = acc[16:32]
        enc = (acc * jax.nn.sigmoid(acc)).astype(BF).astype(F32)
        z_ok = jnp.logical_and(n + dz - 1 >= 0, n + dz - 1 < NN)
        for dx in range(3):
            x_ok = jnp.logical_and(w + dx - 1 >= 0, w + dx - 1 < NW)
            keep = jnp.where(jnp.logical_and(x_ok, z_ok), 1, 0)
            cell = enc[16 * dx : 16 * dx + 16]
            cell = jnp.where(jnp.full((16, 64), keep, jnp.int32) == 1, cell, 0.0)
            encx[dx * 3 + dz] = expand(cell)

    @pl.loop(0, 12)
    def _(xh):
        i = (xh + 6) % 8
        dx = (xh + 6) // 8
        for dz, first, count, place in ((0, 96, 32, 0), (1, 0, 128, 2), (2, 0, 32, 10)):
            rows = tab[pl.ds(mult(i * 128 + first, 16), count), :]
            up = dot_nt(rows, encx[dx * 3 + dz]).astype(BF).astype(F32)
            low, high = shifted_lanes(up)
            base = xh * 576 + place * 16
            v[pl.ds(mult(base, 16), count), :] = low.astype(BF)
            v[pl.ds(mult(base + 192, 16), count), :] = up.astype(BF)
            v[pl.ds(mult(base + 384, 16), count), :] = high.astype(BF)

    for copy in cot_copies:
        copy.wait_recv()

    @pl.loop(0, 10)
    def _(xh):
        pre = dot_nn(t1[...], v[pl.ds(mult(xh * 576, 16), 1728), :])
        grad = (cot_p[xh].astype(F32) * silu_slope(pre)).astype(BF).astype(F32)
        x_edge = jnp.logical_or(
            jnp.logical_and(w == 0, xh == 0), jnp.logical_and(w == NW - 1, xh == 9)
        )
        z_row = iota((160, 128), 0) // 16
        low_row = jnp.where(n == 0, 0, -1)
        high_row = jnp.where(n == NN - 1, 9, -1)
        edge = jnp.full((160, 128), jnp.where(x_edge, 1, 0), jnp.int32)
        drop = (z_row == low_row) | (z_row == high_row) | (edge == 1)
        grad = jnp.where(drop, 0.0, grad)
        low, high = shifted_lanes(grad)
        base = xh * 480
        dg[pl.ds(mult(base, 16), 160), :] = low.astype(BF)
        dg[pl.ds(mult(base + 160, 16), 160), :] = grad.astype(BF)
        dg[pl.ds(mult(base + 320, 16), 160), :] = high.astype(BF)

    gacc[...] = jnp.zeros((128, 1792), F32)

    @pl.loop(0, 8)
    def _(x):
        rows = dg[pl.ds(mult((x + 1) * 480 + 176, 16), 128), :]
        taps = v[pl.ds(mult((x + 1) * 576, 16), 1728), :]
        gacc[:, 0:1728] += dot_nt(rows, taps)

    total = gacc[0:16, :]
    for z in range(1, 8):
        total = total + pltpu.roll(gacc[16 * z : 16 * z + 16, :], 1792 - 16 * z, 1)
    pieces = [total[:, 192 * i + 16 : 192 * i + 64] for i in range(9)]
    pieces.append(jnp.zeros((16, 80), F32))
    packed = jnp.concatenate(pieces, axis=1)
    for p in range(8):
        h1s[p] = packed[8 * (p // 4) : 8 * (p // 4) + 8, 128 * (p % 4) : 128 * (p % 4) + 128]
    h1r[quad] = h1s[quad]

    def h1_copy(d):
        p = (quad + d) % 8
        return remote(
            h1s.at[p], h1r.at[quad], h1_ss.at[d], h1_rs.at[d], {"wide": p * 4 + seat, "narrow": n}
        )

    @pl.loop(1, 8)
    def _(d):
        h1_copy(d).start()

    @pl.loop(0, 8)
    def _(x):
        back = dot_nn(t2[...], dg[pl.ds(mult(x * 480, 16), 1440), :])
        grad = (cot_p[x + 1, 16:144, :].astype(F32) + back).astype(BF)
        for q in range(4):
            ug[x * 4 + q] = grad[32 * q : 32 * q + 32]

    def ug_copy(d):
        t = (w + d) % NW
        return remote(ug.at[t], ur.at[w], ug_ss.at[d], ug_rs.at[d], {"wide": t, "narrow": n})

    @pl.loop(1, NW)
    def _(d):
        ug_copy(d).start()

    ur[w] = ug[w]

    mixed = dot_tn(ug[...].reshape(1024, 128), tab[...])
    mask = (iota((128, 512), 0) % 8) == (iota((128, 512), 1) // 64)
    mixed = jnp.where(mask, mixed, 0.0)
    folded = mixed[:, 0:64]
    for k in range(1, 8):
        folded = folded + mixed[:, 64 * k : 64 * k + 64]
    enc_grad = jnp.sum(folded.reshape(16, 8, 64), axis=1).astype(BF).astype(F32)
    pre_grad = (enc_grad * silu_slope(enc_pre_own)).astype(BF)
    es[...] = pre_grad
    eg[n + 1, pl.ds(mult(w * 16, 16), 16), :] = pre_grad

    def e1_copy(d):
        return remote(
            es,
            eg.at[n + 1, pl.ds(mult(w * 16, 16), 16), :],
            e1_ss.at[d],
            e1_rs.at[d],
            {"wide": (w + d) % NW, "narrow": n},
        )

    @pl.loop(1, NW)
    def _(d):
        e1_copy(d).start()

    @pl.loop(1, 8)
    def _(d):
        h1_copy(d).wait_recv()

    h2s[...] = jnp.sum(h1r[...], axis=0)
    h2r[seat] = h2s[...]

    def h2_copy(d):
        t = quad * 4 + (seat + d) % 4
        return remote(h2s, h2r.at[seat], h2_ss.at[d], h2_rs.at[d], {"wide": t, "narrow": n})

    @pl.loop(1, 4)
    def _(d):
        h2_copy(d).start()

    acc = jnp.zeros((512, 64), F32)
    for a in range(3):
        for b in range(3):
            acc = acc + dot_nt(de[n + 1 + b, 16 + 16 * a : 528 + 16 * a, :], we[3 * a + b])
    encf[...] = (acc * jax.nn.sigmoid(acc)).astype(BF)

    @pl.loop(1, NW)
    def _(d):
        e1_copy(d).wait_recv()

    def e2_copy(d):
        return remote(
            eg.at[n + 1], eg.at[n + 1], e2_ss.at[d], e2_rs.at[d], {"wide": w, "narrow": (n + d) % NN}
        )

    @pl.loop(1, NN)
    def _(d):
        e2_copy(d).start()

    @pl.loop(1, 4)
    def _(d):
        h2_copy(d).wait_recv()

    h3s[...] = jnp.sum(h2r[...], axis=0)
    h3r[n] = h3s[...]

    def h3_copy(d):
        return remote(
            h3s, h3r.at[n], h3_ss.at[d], h3_rs.at[d], {"wide": w, "narrow": (n + d) % NN}
        )

    @pl.loop(1, NN)
    def _(d):
        h3_copy(d).start()

    @pl.loop(1, NW)
    def _(d):
        ug_copy(d).wait_recv()

    def up_step(x, total):
        cells = encf[pl.ds(mult(x * 16, 16), 16), :].astype(F32)
        return total + dot_nn(ur[x], expand(cells))

    up_total = lax.fori_loop(0, NW, up_step, jnp.zeros((32, 512), F32))
    for p in range(8):
        gp[p] = up_total[16 * (p // 4) : 16 * (p // 4) + 16, 128 * (p % 4) : 128 * (p % 4) + 128]
    gr[n] = gp[n]

    def gp_copy(d):
        t = (n + d) % NN
        return remote(gp.at[t], gr.at[n], gp_ss.at[d], gp_rs.at[d], {"wide": w, "narrow": t})

    @pl.loop(1, NN)
    def _(d):
        gp_copy(d).start()

    @pl.loop(1, NN)
    def _(d):
        h3_copy(d).wait_recv()

    h4s[...] = jnp.sum(h3r[...], axis=0)
    h4r[quad] = h4s[...]

    def h4_copy(d):
        t = ((quad + d) % 8) * 4 + seat
        return remote(h4s, h4r.at[quad], h4_ss.at[d], h4_rs.at[d], {"wide": t, "narrow": n})

    @pl.loop(1, 8)
    def _(d):
        h4_copy(d).start()

    @pl.loop(1, NN)
    def _(d):
        e2_copy(d).wait_recv()

    for b in range(3):
        ee[b, 16:528, :] = shifted_rows(eg[n + b].astype(F32))
    acc = jnp.zeros((512, 64), F32)
    for a in range(3):
        for b in range(3):
            acc = acc + dot_nn(ee[b, 16 * a : 16 * a + 512, :], wd[3 * a + b])
    gd_out[...] = acc

    ga[...] = jnp.zeros((3, 192, 192), F32)

    @pl.loop(0, NN)
    def _(z):
        stack = jnp.concatenate([eg[z + 2], eg[z + 1], eg[z]], axis=1)
        for a in range(3):
            ga[a] += dot_tn(stack, de[z + 2, 16 + 16 * a : 528 + 16 * a, :])

    coarse_scale = 1.0 / 64.0
    for a in range(3):
        for b in range(3):
            for e in range(3):
                ge_out[9 * a + 3 * b + e] = (
                    ga[a, 64 * b : 64 * b + 64, 64 * e : 64 * e + 64] * coarse_scale
                )

    @pl.loop(1, NN)
    def _(d):
        gp_copy(d).wait_recv()

    up_sum = jnp.sum(gr[...], axis=0) * coarse_scale
    gu_out[0] = up_sum[:, 0:64]
    gu_out[1] = up_sum[:, 64:128]

    @pl.loop(1, 8)
    def _(d):
        h4_copy(d).wait_recv()

    fine_scale = 1.0 / math.sqrt(2097152.0)
    for p in range(8):
        gw_out[8 * (p // 4) : 8 * (p // 4) + 8, 128 * (p % 4) : 128 * (p % 4) + 128] = (
            h4r[p] * fine_scale
        )

    for copy in cot_copies:
        copy.wait_send()

    @pl.loop(1, NN)
    def _(d):
        dark_copy(d).wait_send()
        e2_copy(d).wait_send()
        gp_copy(d).wait_send()
        h3_copy(d).wait_send()
        h1_copy(d).wait_send()
        h4_copy(d).wait_send()

    @pl.loop(1, 4)
    def _(d):
        h2_copy(d).wait_send()

    @pl.loop(1, NW)
    def _(d):
        ug_copy(d).wait_send()
        e1_copy(d).wait_send()


def on_device(dark, w_enc, up_weight, w_dec, cotangent):
    dark_q = dark.transpose(1, 2, 3, 0).reshape(512, 64)
    taps = w_enc.reshape(9, 3, CH, CH)
    we = taps.transpose(0, 2, 1, 3).reshape(9, CH, 3 * CH)
    wd = w_enc[::-1].reshape(9, 3 * CH, CH)
    tab = up_weight.reshape(64, 8, FCH, CH).transpose(0, 2, 1, 3).reshape(1024, 512)
    dec = w_dec.reshape(3, 3, 3, FCH, FCH)
    fwd = dec.transpose(3, 0, 2, 1, 4).reshape(FCH, 9, 48)
    t1 = jnp.stack(
        [jnp.pad(fwd, ((0, 0), (0, 0), (16 * z, 144 - 16 * z))) for z in range(10)], 0
    ).reshape(160, 1728)
    bwd = dec[::-1, ::-1, ::-1].transpose(4, 0, 2, 1, 3).reshape(FCH, 9, 48)
    t2 = jnp.stack(
        [jnp.pad(bwd, ((0, 0), (0, 0), (16 * z, 112 - 16 * z))) for z in range(8)], 0
    ).reshape(128, 1440)
    cot = cotangent.transpose(1, 2, 0, 3).reshape(8, 128, 128)
    vmem = pl.BlockSpec(memory_space=pltpu.VMEM)
    dma = pltpu.SemaphoreType.DMA
    gd, ge, gu, gw = pl.pallas_call(
        kernel,
        name="step",
        out_shape=(
            jax.ShapeDtypeStruct((512, 64), F32),
            jax.ShapeDtypeStruct((27, 64, 64), F32),
            jax.ShapeDtypeStruct((2, 16, 64), F32),
            jax.ShapeDtypeStruct((16, 512), F32),
        ),
        in_specs=[vmem] * 7,
        out_specs=(vmem,) * 4,
        scratch_shapes=[
            pltpu.VMEM((8, 512, 64), BF),
            pltpu.VMEM((12, 576, 192), BF),
            pltpu.VMEM((10, 160, 128), BF),
            pltpu.VMEM((9, 128, 512), BF),
            pltpu.VMEM((6912, 128), BF),
            pltpu.VMEM((4800, 128), BF),
            pltpu.VMEM((128, 1792), F32),
            pltpu.VMEM((32, 32, 128), BF),
            pltpu.VMEM((32, 32, 128), BF),
            pltpu.VMEM((16, 64), BF),
            pltpu.VMEM((10, 512, 64), BF),
            pltpu.VMEM((3, 544, 192), BF),
            pltpu.VMEM((512, 64), BF),
            pltpu.VMEM((3, 192, 192), F32),
            pltpu.VMEM((8, 16, 128), F32),
            pltpu.VMEM((8, 16, 128), F32),
            pltpu.VMEM((8, 8, 128), F32),
            pltpu.VMEM((8, 8, 128), F32),
            pltpu.VMEM((8, 128), F32),
            pltpu.VMEM((4, 8, 128), F32),
            pltpu.VMEM((8, 128), F32),
            pltpu.VMEM((8, 8, 128), F32),
            pltpu.VMEM((8, 128), F32),
            pltpu.VMEM((8, 8, 128), F32),
            dma((8,)), dma((8,)), dma((8,)), dma((8,)),
            dma((32,)), dma((32,)), dma((32,)), dma((32,)), dma((8,)), dma((8,)),
            dma((8,)), dma((8,)), dma((8,)), dma((8,)), dma((4,)), dma((4,)),
            dma((8,)), dma((8,)), dma((8,)), dma((8,)),
        ],
        compiler_params=pltpu.CompilerParams(
            collective_id=0, has_side_effects=True, vmem_limit_bytes=60000000
        ),
    )(dark_q, we, wd, tab, t1, t2, cot)
    grad_dark = gd.reshape(32, 1, 16, 64).transpose(3, 0, 1, 2)
    grad_dec = (
        gw[:, :432].reshape(FCH, 3, 3, 3, FCH).transpose(1, 3, 2, 0, 4).reshape(27, FCH, FCH)
    )
    return grad_dark, ge, gu, grad_dec


def solution(mesh):
    in_specs = (P(None, None, "narrow", None), P(), P(), P(), P(None, "wide", "narrow", None))
    out_specs = (P(None, None, "narrow", None), P(), P(("wide", "narrow"), None, None), P())
    return jax.shard_map(
        on_device, mesh=mesh, in_specs=in_specs, out_specs=out_specs, check_vma=False
    )
```

```python
import math

import jax
import jax.numpy as jnp
from jax import lax
from jax.experimental import pallas as pl
from jax.experimental.pallas import tpu as pltpu
from jax.sharding import PartitionSpec as P

MESH = pl.DeviceIdType.MESH
BF = jnp.bfloat16
F32 = jnp.float32
NW = 32
NN = 8
RATIO = 8
CH = 64
FCH = 16


def dot_nt(a, b):
    return lax.dot_general(a, b, (((1,), (1,)), ((), ())), preferred_element_type=F32)


def dot_nn(a, b):
    return lax.dot_general(a, b, (((1,), (0,)), ((), ())), preferred_element_type=F32)


def dot_tn(a, b):
    return lax.dot_general(a, b, (((0,), (0,)), ((), ())), preferred_element_type=F32)


def silu_slope(values):
    sigma = jax.nn.sigmoid(values)
    return sigma * (1.0 + values * (1.0 - sigma))


def iota(shape, dim):
    return lax.broadcasted_iota(jnp.int32, shape, dim)


def mult(value, of):
    return pl.multiple_of(value, of)


def shifted_rows(field):
    rows = field.shape[0]
    y = iota(field.shape, 0) % 16
    low = jnp.where(y == 0, 0.0, pltpu.roll(field, 1, 0))
    high = jnp.where(y == 15, 0.0, pltpu.roll(field, rows - 1, 0))
    return jnp.concatenate([low, field, high], axis=1).astype(BF)


def shifted_lanes(field):
    lane = iota(field.shape, 1)
    low = jnp.where(lane == 0, 0.0, pltpu.roll(field, 1, 1))
    high = jnp.where(lane == 127, 0.0, pltpu.roll(field, 127, 1))
    return low, high


def expand(enc):
    rep = jnp.broadcast_to(enc[:, None, :], (16, 8, 64)).reshape(128, 64)
    wide = jnp.concatenate([rep] * 8, axis=1)
    mask = (iota((128, 512), 0) % 8) == (iota((128, 512), 1) // 64)
    return jnp.where(mask, wide, 0.0).astype(BF)


def remote(src, dst, send, recv, target):
    return pltpu.make_async_remote_copy(
        src_ref=src, dst_ref=dst, send_sem=send, recv_sem=recv, device_id=target, device_id_type=MESH
    )


class Exchange:
    def __init__(self, copy, count, pending):
        self.copy = copy
        self.count = count
        self.pending = pending
        self.landed = False

    def each(self, act):
        @pl.loop(1, self.count)
        def _(d):
            act(self.copy(d))

    def start(self):
        self.pending.append(self)
        self.each(lambda c: c.start())

    def wait_recv(self):
        self.landed = True
        self.each(lambda c: c.wait_recv())

    def finish(self):
        if not self.landed:
            self.wait_recv()
        self.each(lambda c: c.wait_send())


def kernel(
    dark, wenc, uw, wdec, wdec_t, cot,
    gd_out, ge_out, gu_out, gw_out,
    rows_f, cot_f, we, wd, tab, t1, t2, cot_o,
    dark_pad, dark_w, dew, dark_p, de, e1r, eg_p, cot_p, encx, v, dg, gacc, ug, ur, es, eg, ee, encf, ga, gp, gr,
    h1s, h1r, h2s, h2r, h3s, h3r, h4s, h4r,
    win_ss, win_rs, dark_ss, dark_rs, dr_ss, dr_rs, er_ss, er_rs, cot_ss, cot_rs, ug_ss, ug_rs, e1_ss, e1_rs, e2_ss, e2_rs,
    gp_ss, gp_rs, h1_ss, h1_rs, h2_ss, h2_rs, h3_ss, h3_rs, h4_ss, h4_rs,
):
    w = lax.axis_index("wide")
    n = lax.axis_index("narrow")
    wl, wr = (w + NW - 1) % NW, (w + 1) % NW
    nl, nr = (n + NN - 1) % NN, (n + 1) % NN
    quad = w // 4
    seat = w % 4
    pending = []
    cot_copies = []
    win_copies = []

    def finish():
        for exchange in pending:
            exchange.finish()
        for copy in cot_copies:
            copy.wait_send()
        for copy in win_copies:
            copy.wait_send()

    barrier = pltpu.get_barrier_semaphore()

    def greet(target):
        pl.semaphore_signal(barrier, inc=1, device_id=target, device_id_type=MESH)

    @pl.loop(1, NN)
    def _(d):
        greet({"wide": w, "narrow": (n + d) % NN})

    for a in (wl, wr):
        for b in (nl, nr):
            greet({"wide": a, "narrow": b})

    @pl.loop(1, NW)
    def _(d):
        greet({"wide": (w + d) % NW, "narrow": n})

    cot_f[...] = cot[...].astype(F32)

    @pl.loop(0, 8)
    def _(x):
        for z in range(8):
            rows = cot_f[pl.ds(x * 8 + z, 16, stride=64), :].astype(BF)
            cot_o[x, 16 * z : 16 * z + 16, :] = rows
            cot_p[x + 1, 16 * z + 16 : 16 * z + 32, :] = rows

    core = w % 2
    mate = w + 1 - 2 * core
    dark_pad[0:32, :] = jnp.zeros((32, 64), BF)
    dark_pad[32:544, :] = dark[...]
    dark_pad[544:576, :] = jnp.zeros((32, 64), BF)
    pair = dark[...].reshape(16, 32, 64)
    dark_p[n] = jnp.concatenate([pair[:, 0:16], pair[:, 16:32]], axis=2).reshape(256, 128)
    dark_w[2] = dark_pad[pl.ds(mult(w * 16, 16), 80), :]
    for i in (0, 1, 10, 11):
        de[i] = jnp.zeros((544, 192), BF)

    @pl.loop(2, 10)
    def _(i):
        de[i, 0:16, :] = jnp.zeros((16, 192), BF)
        de[i, 528:544, :] = jnp.zeros((16, 192), BF)

    zero_coarse = jnp.zeros((512, 64), BF)
    eg[0] = zero_coarse
    eg[9] = zero_coarse
    for i in range(3):
        ee[i, 0:16, :] = jnp.zeros((16, 192), BF)
        ee[i, 528:544, :] = jnp.zeros((16, 192), BF)

    for i in range(9):
        we[i] = jnp.concatenate([wenc[3 * i + e] for e in range(3)], axis=1)
        for e in range(3):
            wd[i, 64 * e : 64 * e + 64, :] = wenc[26 - 3 * i - e]

    def spread(get, block, count, out):
        zeros = jnp.zeros((16, block - 48), F32)
        parts = []
        for a in range(3):
            for e in range(3):
                parts += [get(a, b, e).astype(F32) for b in range(3)] + [zeros]
        pad = -9 * block % 128
        if pad:
            parts.append(jnp.zeros((16, pad), F32))
        base = jnp.concatenate(parts, axis=1)
        for z in range(count):
            row = base if z == 0 else pltpu.roll(base, 16 * z, 1)
            out[16 * z : 16 * z + 16, :] = row[:, 0 : 9 * block].astype(BF)

    spread(lambda a, b, e: wdec[9 * a + 3 * b + e], 192, 10, t1)
    spread(lambda a, b, e: wdec_t[26 - (9 * a + 3 * b + e)], 160, 8, t2)

    pl.semaphore_wait(barrier, NN - 1 + NW - 1 + 4)

    for index, dz in enumerate((1, -1, 2, -2)):
        win_copies.append(
            remote(
                dark_pad.at[pl.ds(mult(w * 16, 16), 80), :],
                dark_w.at[2 - dz],
                win_ss.at[index],
                win_rs.at[index],
                {"wide": w, "narrow": (n + dz + NN) % NN},
            )
        )
    for copy in win_copies:
        copy.start()

    for dx in (-1, 0, 1):
        for dz in (-1, 0, 1):
            if dx == 0 and dz == 0:
                continue
            tw = (wl, w, wr)[dx + 1]
            tn = (nl, n, nr)[dz + 1]
            sx = {-1: (0, 1), 0: (0, 8), 1: (7, 1)}[dx]
            sz = {-1: (0, 16), 0: (0, 128), 1: (112, 16)}[dz]
            tx = {-1: 9, 0: 1, 1: 0}[dx]
            tz = {-1: 144, 0: 16, 1: 0}[dz]
            index = len(cot_copies)
            cot_copies.append(
                remote(
                    cot_o.at[pl.ds(sx[0], sx[1]), pl.ds(sz[0], sz[1]), :],
                    cot_p.at[pl.ds(tx, sx[1]), pl.ds(tz, sz[1]), :],
                    cot_ss.at[index],
                    cot_rs.at[index],
                    {"wide": tw, "narrow": tn},
                )
            )
    for copy in cot_copies:
        copy.start()
    half = pl.ds(mult(core * 128, 128), 128)

    def dark_copy(d):
        part = dark_p.at[n, half, :]
        return remote(
            part, part, dark_ss.at[d], dark_rs.at[d], {"wide": w, "narrow": (n + d) % NN}
        )

    dark_x = Exchange(dark_copy, NN, pending)
    dark_x.start()

    @pl.loop(0, 16)
    def _(o):
        rows_f[pl.ds(mult(o * 512, 512), 512), 0:64] = uw[o].astype(F32).T

    @pl.loop(0, 64)
    def _(ij):
        parts = [rows_f[pl.ds(ij * 8 + k, 16, stride=512), :][:, 0:64] for k in range(8)]
        tab[pl.ds(mult(ij * 16, 16), 16), :] = jnp.concatenate(parts, axis=1).astype(BF)

    for copy in win_copies:
        copy.wait_recv()
    for i in range(5):
        plane = n + i - 2
        inside = jnp.where(jnp.logical_and(plane >= 0, plane < NN), 1, 0)
        field = jnp.where(jnp.full((80, 64), inside, jnp.int32) == 1, dark_w[i].astype(F32), 0.0)
        dew[i] = shifted_rows(field)

    acc = jnp.zeros((144, 64), F32)
    for a in range(3):
        for b in range(3):
            rows = jnp.concatenate([dew[dz + b, 16 * a : 16 * a + 48, :] for dz in range(3)], axis=0)
            acc = acc + dot_nt(rows, we[3 * a + b])
    enc_pre_own = acc[64:80]
    enc = (acc * jax.nn.sigmoid(acc)).astype(BF).astype(F32)
    for dz in range(3):
        z_ok = jnp.logical_and(n + dz - 1 >= 0, n + dz - 1 < NN)
        for dx in range(3):
            x_ok = jnp.logical_and(w + dx - 1 >= 0, w + dx - 1 < NW)
            keep = jnp.where(jnp.logical_and(x_ok, z_ok), 1, 0)
            cell = enc[48 * dz + 16 * dx : 48 * dz + 16 * dx + 16]
            cell = jnp.where(jnp.full((16, 64), keep, jnp.int32) == 1, cell, 0.0)
            encx[dx * 3 + dz] = expand(cell)

    @pl.loop(0, 12)
    def _(xh):
        i = (xh + 6) % 8
        dx = (xh + 6) // 8
        for dz, first, count, place in ((0, 96, 32, 0), (1, 0, 128, 2), (2, 0, 32, 10)):
            rows = tab[pl.ds(mult(i * 128 + first, 16), count), :]
            up = dot_nt(rows, encx[dx * 3 + dz]).astype(BF).astype(F32)
            low, high = shifted_lanes(up)
            base = xh * 576 + place * 16
            v[pl.ds(mult(base, 16), count), :] = low.astype(BF)
            v[pl.ds(mult(base + 192, 16), count), :] = up.astype(BF)
            v[pl.ds(mult(base + 384, 16), count), :] = high.astype(BF)

    def relay(buffer, exchange, sends, lands):
        def copy(d):
            part = buffer.at[(n + NN - d) % NN, half, :]
            return remote(part, part, sends.at[d], lands.at[d], {"wide": mate, "narrow": n})

        passed = Exchange(copy, NN, pending)
        pending.append(passed)
        exchange.landed = True

        @pl.loop(1, NN)
        def _(d):
            exchange.copy(d).wait_recv()
            copy(d).start()

        return passed

    dark_r = relay(dark_p, dark_x, dr_ss, dr_rs)
    for copy in cot_copies:
        copy.wait_recv()

    @pl.loop(0, 10)
    def _(xh):
        pre = dot_nn(t1[...], v[pl.ds(mult(xh * 576, 16), 1728), :])
        grad = (cot_p[xh].astype(F32) * silu_slope(pre)).astype(BF).astype(F32)
        x_edge = jnp.logical_or(
            jnp.logical_and(w == 0, xh == 0), jnp.logical_and(w == NW - 1, xh == 9)
        )
        z_row = iota((160, 128), 0) // 16
        low_row = jnp.where(n == 0, 0, -1)
        high_row = jnp.where(n == NN - 1, 9, -1)
        edge = jnp.full((160, 128), jnp.where(x_edge, 1, 0), jnp.int32)
        drop = (z_row == low_row) | (z_row == high_row) | (edge == 1)
        grad = jnp.where(drop, 0.0, grad)
        low, high = shifted_lanes(grad)
        base = xh * 480
        dg[pl.ds(mult(base, 16), 160), :] = low.astype(BF)
        dg[pl.ds(mult(base + 160, 16), 160), :] = grad.astype(BF)
        dg[pl.ds(mult(base + 320, 16), 160), :] = high.astype(BF)

    gacc[...] = jnp.zeros((128, 1792), F32)

    @pl.loop(0, 8)
    def _(x):
        rows = dg[pl.ds(mult((x + 1) * 480 + 176, 16), 128), :]
        taps = v[pl.ds(mult((x + 1) * 576, 16), 1728), :]
        gacc[:, 0:1728] += dot_nt(rows, taps)

    total = gacc[0:16, :]
    for z in range(1, 8):
        total = total + pltpu.roll(gacc[16 * z : 16 * z + 16, :], 1792 - 16 * z, 1)
    pieces = [total[:, 192 * i + 16 : 192 * i + 64] for i in range(9)]
    pieces.append(jnp.zeros((16, 80), F32))
    packed = jnp.concatenate(pieces, axis=1)
    for p in range(8):
        h1s[p] = packed[8 * (p // 4) : 8 * (p // 4) + 8, 128 * (p % 4) : 128 * (p % 4) + 128]
    h1r[quad] = h1s[quad]

    def h1_copy(d):
        p = (quad + d) % 8
        return remote(
            h1s.at[p], h1r.at[quad], h1_ss.at[d], h1_rs.at[d], {"wide": p * 4 + seat, "narrow": n}
        )

    h1_x = Exchange(h1_copy, 8, pending)
    h1_x.start()

    @pl.loop(0, 8)
    def _(x):
        back = dot_nn(t2[...], dg[pl.ds(mult(x * 480, 16), 1440), :])
        grad = (cot_p[x + 1, 16:144, :].astype(F32) + back).astype(BF)
        for q in range(4):
            ug[x * 4 + q] = grad[32 * q : 32 * q + 32]

    mixed = dot_tn(ug[...].reshape(1024, 128), tab[...])
    mask = (iota((128, 512), 0) % 8) == (iota((128, 512), 1) // 64)
    mixed = jnp.where(mask, mixed, 0.0)
    folded = mixed[:, 0:64]
    for k in range(1, 8):
        folded = folded + mixed[:, 64 * k : 64 * k + 64]
    enc_grad = jnp.sum(folded.reshape(16, 8, 64), axis=1).astype(BF).astype(F32)
    pre_grad = (enc_grad * silu_slope(enc_pre_own)).astype(BF).astype(F32)
    zero_half = jnp.zeros((16, 64), F32)
    even = jnp.concatenate([pre_grad, zero_half], axis=1)
    odd = jnp.concatenate([zero_half, pre_grad], axis=1)
    tile = jnp.where(jnp.full((16, 128), core, jnp.int32) == 0, even, odd).astype(BF)
    es[...] = tile
    e1r[w] = tile

    def e1_copy(d):
        return remote(
            es, e1r.at[w], e1_ss.at[d], e1_rs.at[d], {"wide": (w + d) % NW, "narrow": n}
        )

    e1_x = Exchange(e1_copy, NW, pending)
    e1_x.start()

    def ug_copy(d):
        t = (w + d) % NW
        return remote(ug.at[t], ur.at[w], ug_ss.at[d], ug_rs.at[d], {"wide": t, "narrow": n})

    ug_x = Exchange(ug_copy, NW, pending)
    ug_x.start()

    ur[w] = ug[w]

    h1_x.wait_recv()

    h2s[...] = jnp.sum(h1r[...], axis=0)
    h2r[seat] = h2s[...]

    def h2_copy(d):
        t = quad * 4 + (seat + d) % 4
        return remote(h2s, h2r.at[seat], h2_ss.at[d], h2_rs.at[d], {"wide": t, "narrow": n})

    h2_x = Exchange(h2_copy, 4, pending)
    h2_x.start()

    dark_r.wait_recv()

    def unpack(plane):
        both = plane.reshape(16, 16, 128)
        return jnp.stack([both[:, :, 0:64], both[:, :, 64:128]], axis=1).reshape(512, 64)

    @pl.loop(0, NN)
    def _(z):
        de[z + 2, 16:528, :] = shifted_rows(unpack(dark_p[z].astype(F32)))

    acc = jnp.zeros((512, 64), F32)
    for a in range(3):
        for b in range(3):
            acc = acc + dot_nt(de[n + 1 + b, 16 * a : 512 + 16 * a, :], we[3 * a + b])
    encf[...] = (acc * jax.nn.sigmoid(acc)).astype(BF)

    e1_x.wait_recv()

    for m in range(16):
        eg_p[n, 16 * m : 16 * m + 16, :] = (
            e1r[2 * m].astype(F32) + e1r[2 * m + 1].astype(F32)
        ).astype(BF)

    def e2_copy(d):
        part = eg_p.at[n, half, :]
        return remote(part, part, e2_ss.at[d], e2_rs.at[d], {"wide": w, "narrow": (n + d) % NN})

    e2_x = Exchange(e2_copy, NN, pending)
    e2_x.start()

    h2_x.wait_recv()

    h3s[...] = jnp.sum(h2r[...], axis=0)
    h3r[n] = h3s[...]

    def h3_copy(d):
        return remote(
            h3s, h3r.at[n], h3_ss.at[d], h3_rs.at[d], {"wide": w, "narrow": (n + d) % NN}
        )

    h3_x = Exchange(h3_copy, NN, pending)
    h3_x.start()

    ug_x.wait_recv()

    def up_step(x, total):
        cells = encf[pl.ds(mult(x * 16, 16), 16), :].astype(F32)
        return total + dot_nn(ur[x], expand(cells))

    up_total = lax.fori_loop(0, NW, up_step, jnp.zeros((32, 512), F32))
    for p in range(8):
        gp[p] = up_total[16 * (p // 4) : 16 * (p // 4) + 16, 128 * (p % 4) : 128 * (p % 4) + 128]
    gr[n] = gp[n]

    def gp_copy(d):
        t = (n + d) % NN
        return remote(gp.at[t], gr.at[n], gp_ss.at[d], gp_rs.at[d], {"wide": w, "narrow": t})

    gp_x = Exchange(gp_copy, NN, pending)
    gp_x.start()

    h3_x.wait_recv()

    h4s[...] = jnp.sum(h3r[...], axis=0)
    h4r[quad] = h4s[...]

    def h4_copy(d):
        t = ((quad + d) % 8) * 4 + seat
        return remote(h4s, h4r.at[quad], h4_ss.at[d], h4_rs.at[d], {"wide": t, "narrow": n})

    h4_x = Exchange(h4_copy, 8, pending)
    h4_x.start()

    eg_r = relay(eg_p, e2_x, er_ss, er_rs)
    eg_r.wait_recv()

    @pl.loop(0, NN)
    def _(z):
        eg[z + 1] = unpack(eg_p[z].astype(F32)).astype(BF)


    for b in range(3):
        ee[b, 16:528, :] = shifted_rows(eg[n + b].astype(F32))
    acc = jnp.zeros((512, 64), F32)
    for a in range(3):
        for b in range(3):
            acc = acc + dot_nn(ee[b, 16 * a : 16 * a + 512, :], wd[3 * a + b])
    gd_out[...] = acc

    ga[...] = jnp.zeros((3, 192, 192), F32)

    @pl.loop(0, NN)
    def _(z):
        stack = jnp.concatenate([eg[z + 2], eg[z + 1], eg[z]], axis=1)
        for a in range(3):
            ga[a] += dot_tn(stack, de[z + 2, 16 * a : 512 + 16 * a, :])

    coarse_scale = 1.0 / 64.0
    for a in range(3):
        for b in range(3):
            for e in range(3):
                ge_out[9 * a + 3 * b + e] = (
                    ga[a, 64 * b : 64 * b + 64, 64 * e : 64 * e + 64] * coarse_scale
                )

    gp_x.wait_recv()

    up_sum = jnp.sum(gr[...], axis=0) * coarse_scale
    gu_out[0] = up_sum[:, 0:64]
    gu_out[1] = up_sum[:, 64:128]

    h4_x.wait_recv()

    fine_scale = 1.0 / math.sqrt(2097152.0)
    top = jnp.concatenate([h4r[p] for p in range(4)], axis=1)
    low = jnp.concatenate([h4r[p] for p in range(4, 8)], axis=1)
    dec = jnp.concatenate([top, low], axis=0) * fine_scale
    for a in range(3):
        for b in range(3):
            for e in range(3):
                place = 144 * a + 48 * e + 16 * b
                gw_out[9 * a + 3 * b + e] = dec[:, place : place + 16]

    finish()


def on_device(dark, w_enc, up_weight, w_dec, cotangent):
    dark_q = dark.transpose(1, 2, 3, 0).reshape(512, 64)
    up_rows = up_weight.transpose(1, 2, 0)
    cot = cotangent.reshape(1024, 128)
    vmem = pl.BlockSpec(memory_space=pltpu.VMEM)
    dma = pltpu.SemaphoreType.DMA
    gd, ge, gu, gw = pl.pallas_call(
        kernel,
        name="step",
        out_shape=(
            jax.ShapeDtypeStruct((512, 64), F32),
            jax.ShapeDtypeStruct((27, 64, 64), F32),
            jax.ShapeDtypeStruct((2, 16, 64), F32),
            jax.ShapeDtypeStruct((27, 16, 16), F32),
        ),
        in_specs=[vmem] * 6,
        out_specs=(vmem,) * 4,
        scratch_shapes=[
            pltpu.VMEM((8192, 128), F32),
            pltpu.VMEM((1024, 128), F32),
            pltpu.VMEM((9, 64, 192), BF),
            pltpu.VMEM((9, 192, 64), BF),
            pltpu.VMEM((1024, 512), BF),
            pltpu.VMEM((160, 1728), BF),
            pltpu.VMEM((128, 1440), BF),
            pltpu.VMEM((8, 128, 128), BF),
            pltpu.VMEM((576, 64), BF),
            pltpu.VMEM((5, 80, 64), BF),
            pltpu.VMEM((5, 80, 192), BF),
            pltpu.VMEM((8, 256, 128), BF),
            pltpu.VMEM((12, 544, 192), BF),
            pltpu.VMEM((32, 16, 128), BF),
            pltpu.VMEM((8, 256, 128), BF),
            pltpu.VMEM((10, 160, 128), BF),
            pltpu.VMEM((9, 128, 512), BF),
            pltpu.VMEM((6912, 128), BF),
            pltpu.VMEM((4800, 128), BF),
            pltpu.VMEM((128, 1792), F32),
            pltpu.VMEM((32, 32, 128), BF),
            pltpu.VMEM((32, 32, 128), BF),
            pltpu.VMEM((16, 128), BF),
            pltpu.VMEM((10, 512, 64), BF),
            pltpu.VMEM((3, 544, 192), BF),
            pltpu.VMEM((512, 64), BF),
            pltpu.VMEM((3, 192, 192), F32),
            pltpu.VMEM((8, 16, 128), F32),
            pltpu.VMEM((8, 16, 128), F32),
            pltpu.VMEM((8, 8, 128), F32),
            pltpu.VMEM((8, 8, 128), F32),
            pltpu.VMEM((8, 128), F32),
            pltpu.VMEM((4, 8, 128), F32),
            pltpu.VMEM((8, 128), F32),
            pltpu.VMEM((8, 8, 128), F32),
            pltpu.VMEM((8, 128), F32),
            pltpu.VMEM((8, 8, 128), F32),
            dma((4,)), dma((4,)), dma((8,)), dma((8,)), dma((8,)), dma((8,)), dma((8,)), dma((8,)),
            dma((8,)), dma((8,)),
            dma((32,)), dma((32,)), dma((32,)), dma((32,)), dma((8,)), dma((8,)),
            dma((8,)), dma((8,)), dma((8,)), dma((8,)), dma((4,)), dma((4,)),
            dma((8,)), dma((8,)), dma((8,)), dma((8,)),
        ],
        compiler_params=pltpu.CompilerParams(
            collective_id=0, has_side_effects=True, vmem_limit_bytes=60000000
        ),
    )(dark_q, w_enc, up_rows, w_dec, w_dec.transpose(0, 2, 1), cot)
    grad_dark = gd.reshape(32, 1, 16, 64).transpose(3, 0, 1, 2)
    return grad_dark, ge, gu, gw


def solution(mesh):
    in_specs = (P(None, None, "narrow", None), P(), P(), P(), P(None, "wide", "narrow", None))
    out_specs = (P(None, None, "narrow", None), P(), P(("wide", "narrow"), None, None), P())
    return jax.shard_map(
        on_device, mesh=mesh, in_specs=in_specs, out_specs=out_specs, check_vma=False
    )
```
